32 devices in a mesh: row: 8 (over z, y), col: 4 (over x, core).
Axes of the slice: x: 2, y: 2, z: 4, core: 2. Of those that a mesh axis runs over, the one named last changes fastest.
Arguments:
- ancestor: float32 [1024, 1024], P('row', 'col'), may hold values from -0.1875 to 0.1875
- factor: float32 [1024, 16, 128], P(('row', 'col')), may hold values from -1.5 to 1.5
- diag_inv: float32 [16, 128, 128], replicated, may hold values from -6 to 6
- structure: int32 [16, 96], replicated, may hold values from 0 to 127, as said below
Outputs:
- inverse_panel: float32 [1024, 16, 128], P(('row', 'col'))
- inverse_diagonal: float32 [16, 128, 128], replicated
The draws below stay inside these ranges and needn't reach their ends.
Inputs may be any that keep to these rules, and one draw needn't show every extreme that they name: Each row of structure lists 96 different block numbers, in no particular order.
All inputs are finite; a program needn't handle non-finite values.
Results may differ from the reference program's by a relative error of at most 0.00007.
Values sent between devices are 32-bit elements; how exact they have to be, the bound alone decides.
A program may use at most 64 MiB of HBM per device.

```python
import jax
import jax.numpy as jnp
from jax import lax

W = 128
SIB = 16
RB = 8
NA = 1024
NBLK = 128
NSEL = 96


def draw_structure(key, part):
    sibling_keys = jax.random.split(jax.random.fold_in(key, 11), SIB)
    orders = jax.vmap(lambda single_key: jax.random.permutation(single_key, NBLK))(sibling_keys)
    return orders[:, :NSEL].astype(jnp.int32)


def block_scale(own_key, extent, cuts, low, high):
    def one(axis_at, parts):
        steps = jax.random.uniform(jax.random.fold_in(jax.random.fold_in(own_key, 6), axis_at), (parts,), jnp.float32, low / len(cuts), high / len(cuts))
        return jnp.repeat(jnp.exp(steps), extent[axis_at] // parts).reshape((-1,) + (1,) * (len(extent) - axis_at - 1))

    gain = one(*cuts[0])
    for cut in cuts[1:]:
        gain = gain * one(*cut)
    return gain


def bell_draw(key, dims, spread, limit, pieces=(), held_as=jnp.bfloat16):
    loudness = block_scale(key, dims, pieces, -0.22, 0.18) if pieces else 1.0
    values = jax.random.normal(key, dims, jnp.float32) * spread * loudness
    return jnp.minimum(jnp.maximum(values, -limit), limit).astype(held_as)


def setup_inputs(seed: int = 0) -> dict:
    keys = jax.random.split(jax.random.key(seed), 5)
    ancestor = bell_draw(keys[0], (NA, NA), NA ** -0.5, 0.1875, ((0, 8), (1, 4)), jnp.float32)
    factor = bell_draw(keys[1], (NA, SIB, W), 0.25, 1.5, ((0, 32),), jnp.float32)
    diag_inv = bell_draw(keys[2], (SIB, W, W), 1.0, 6.0, (), jnp.float32)
    structure = draw_structure(jax.random.fold_in(keys[4], 71), 0)
    return {"ancestor": ancestor, "factor": factor, "diag_inv": diag_inv, "structure": structure}


def reference(ancestor, factor, diag_inv, structure):
    sibling_ids = jnp.arange(SIB, dtype=jnp.int32)[:, None]
    block_mask = jnp.zeros((SIB, NBLK), jnp.float32).at[sibling_ids, structure].set(1.0)
    row_mask = jnp.repeat(block_mask, RB, axis=1).T
    masked = factor * row_mask[:, :, None]
    product = jnp.dot(ancestor, masked.reshape(NA, SIB * W), precision=lax.Precision.HIGHEST, preferred_element_type=jnp.float32)
    panel = -product.reshape(NA, SIB, W) * row_mask[:, :, None]
    update = jnp.einsum("bsw,bsv->swv", masked, panel, precision=lax.Precision.HIGHEST)
    return panel, diag_inv - update
```

```python
import functools

import jax
import jax.numpy as jnp
from jax import lax
from jax.experimental import pallas as pl
from jax.experimental.pallas import tpu as pltpu
from jax.sharding import PartitionSpec as P

RB = 8
MESH = pl.DeviceIdType.MESH
HIGHEST = lax.Precision.HIGHEST


def kernel(
    line, group, lows, cols,
    a_ref, m_ref, c_out, u_out,
    a_full, b_buf, c_buf, u_part, u_recv,
    local_sem, a_send, a_recv, b_send, b_recv, z_send,
    c_send, c_recv, r_send, r_recv, l_send, u_send, u_recv_sem,
):
    row, col = lax.axis_index("row"), lax.axis_index("col")
    h, p = row // lows, (row % lows) * cols + col
    rows, width = m_ref.shape[1], m_ref.shape[2]
    slab = group * rows
    chunk = u_recv.shape[1]
    sib_width = u_part.shape[1]
    per = width // sib_width
    me = h * group + p

    def dev(hq, pq):
        return (hq * lows + pq // cols, pq % cols)

    def remote(src, dst, send, recv, target):
        return pltpu.make_async_remote_copy(
            src_ref=src, dst_ref=dst, send_sem=send, recv_sem=recv,
            device_id=target, device_id_type=MESH,
        )

    def peer(k, n, own):
        return lax.rem(own + k, n)

    def each_plane(body):
        def step(k, carry):
            body(k, peer(k, group, p))
            return carry
        lax.fori_loop(1, group, step, 0)

    def each_line(body):
        def step(k, carry):
            body(k, peer(k, line, h))
            return carry
        lax.fori_loop(1, line, step, 0)

    barrier = pltpu.get_barrier_semaphore()
    each_plane(lambda k, q: pl.semaphore_signal(
        barrier, inc=1, device_id=dev(h, q), device_id_type=MESH))
    each_line(lambda k, hq: pl.semaphore_signal(
        barrier, inc=1, device_id=dev(hq, p), device_id_type=MESH))
    pl.semaphore_wait(barrier, group + line - 2)

    def piece(hs, q):
        return b_buf.at[pl.ds(pl.multiple_of((hs * group + q) * rows, rows), rows)]

    def b_copy(k, q):
        return remote(m_ref.at[q], piece(h, p), b_send.at[k], b_recv.at[me], dev(h, q))

    def b_wait(hs, q):
        remote(piece(hs, q), piece(hs, q), b_send.at[0], b_recv.at[hs * group + q],
               dev(h, p)).wait_recv()

    def forward(hs, q, to_right):
        side = 0 if to_right else 1
        target = dev(h + 1, p) if to_right else dev(h - 1, p)
        remote(piece(hs, q), piece(hs, q), z_send.at[side, hs],
               b_recv.at[hs * group + q], target).start()

    def a_copy(k, q):
        return remote(a_ref, a_full.at[p], a_send.at[k], a_recv.at[p], dev(h, q))

    own_a = pltpu.make_async_copy(a_ref, a_full.at[p], local_sem.at[0])
    own_b = pltpu.make_async_copy(m_ref.at[p], piece(h, p), local_sem.at[1])
    own_b.start()
    each_plane(lambda k, q: b_copy(k, q).start())
    own_a.start()
    own_b.wait()

    def first(k, carry):
        q = lax.rem(p + group - k, group)

        @pl.when(k > 0)
        def _():
            b_wait(h, q)

        @pl.when(h + 1 < line)
        def _():
            forward(h, q, True)

        @pl.when(h > 0)
        def _():
            forward(h, q, False)

        @pl.when(k == 0)
        def _():
            each_plane(lambda j, r: a_copy(j, r).start())
        return carry

    lax.fori_loop(0, group, first, 0)

    def relay(t, carry):
        def one(k, inner):
            q = lax.rem(p + group - k, group)

            @pl.when(h >= t)
            def _():
                b_wait(h - t, q)

                @pl.when(h + 1 < line)
                def _():
                    forward(h - t, q, True)

            @pl.when(h + t < line)
            def _():
                b_wait(h + t, q)

                @pl.when(h > 0)
                def _():
                    forward(h + t, q, False)
            return inner
        lax.fori_loop(0, group, one, 0)
        return carry

    lax.fori_loop(1, line - 1, relay, 0)

    c_buf[...] = jnp.zeros_like(c_buf)
    own_a.wait()
    each_plane(lambda k, q: remote(
        a_full.at[q], a_full.at[q], a_send.at[0], a_recv.at[q], dev(h, p)).wait_recv())
    a_rows, depth = a_ref.shape
    step = min(slab, depth)

    def multiply(hs):
        for part in range(slab // step):
            start = hs * slab + part * step
            block = b_buf[pl.ds(pl.multiple_of(start, step), step), :]
            at, off = start // depth, start % depth
            for lo in range(lows):
                if step == depth:
                    left = a_full[lo * cols + at]
                else:
                    left = a_full[lo * cols + at, :, pl.ds(pl.multiple_of(off, step), step)]
                c_buf[lo * a_rows:(lo + 1) * a_rows, :] += jnp.dot(
                    left, block, precision=HIGHEST, preferred_element_type=jnp.float32
                )

    def arrived(hs, carry):
        @pl.when((hs - h < line - 1) & (h - hs < line - 1))
        def _():
            multiply(hs)
        return carry

    lax.fori_loop(0, line, arrived, 0)
    last = line - 1

    @pl.when((h == 0) | (h == last))
    def _():
        far = last - h

        def wait_far(k, carry):
            b_wait(far, lax.rem(p + group - k, group))
            return carry

        lax.fori_loop(0, group, wait_far, 0)
        multiply(far)

    mine = pl.ds(pl.multiple_of(h * slab, slab), slab)
    for s in range(per):
        lanes = slice(s * sib_width, (s + 1) * sib_width)
        u_part[s * sib_width:(s + 1) * sib_width, :] = lax.dot_general(
            b_buf[mine, lanes], c_buf[:, lanes], (((0,), (0,)), ((), ())),
            precision=HIGHEST, preferred_element_type=jnp.float32,
        )

    def r_copy(k, hq):
        return remote(u_part.at[pl.ds(pl.multiple_of(hq * chunk, chunk), chunk)],
                      u_recv.at[h], r_send.at[k], r_recv.at[h], dev(hq, p))

    def c_copy(k, q):
        return remote(c_buf.at[pl.ds(pl.multiple_of(q * rows, rows), rows)], c_out.at[p],
                      c_send.at[k], c_recv.at[p], dev(h, q))

    each_line(lambda k, hq: r_copy(k, hq).start())
    each_plane(lambda k, q: c_copy(k, q).start())
    c_out[p] = c_buf[pl.ds(pl.multiple_of(p * rows, rows), rows), :]
    u_recv[h] = u_part[pl.ds(pl.multiple_of(h * chunk, chunk), chunk), :]
    each_line(lambda k, hq: remote(
        u_recv.at[hq], u_recv.at[hq], r_send.at[0], r_recv.at[hq], dev(h, p)).wait_recv())
    total = u_recv[0]
    for hs in range(1, line):
        total = total + u_recv[hs]

    def u_at(hs, q):
        return pl.ds(pl.multiple_of((q * line + hs) * chunk, chunk), chunk)

    u_out[u_at(h, p), :] = total

    def l_copy(k, hq):
        here = u_out.at[u_at(h, p)]
        return remote(here, here, l_send.at[k], u_recv_sem.at[me], dev(hq, p))

    def u_copy(hs, k, q):
        here = u_out.at[u_at(hs, p)]
        return remote(here, here, u_send.at[hs, k], u_recv_sem.at[hs * group + p], dev(h, q))

    def u_wait(hs, q):
        here = u_out.at[u_at(hs, q)]
        remote(here, here, l_send.at[0], u_recv_sem.at[hs * group + q], dev(h, p)).wait_recv()

    each_line(lambda k, hq: l_copy(k, hq).start())
    each_plane(lambda k, q: u_copy(h, k, q).start())

    def spread(k, hq):
        u_wait(hq, p)
        each_plane(lambda j, q: u_copy(hq, j, q).start())

    each_line(spread)

    each_plane(lambda k, q: b_copy(k, q).wait_send())
    each_plane(lambda k, q: a_copy(k, q).wait_send())
    each_plane(lambda k, q: c_copy(k, q).wait_send())
    each_line(lambda k, hq: r_copy(k, hq).wait_send())
    each_line(lambda k, hq: l_copy(k, hq).wait_send())

    def drain(hs, carry):
        whole = b_buf.at[pl.ds(pl.multiple_of(hs * slab, slab), slab)]

        @pl.when((hs <= h) & (h + 1 < line))
        def _():
            remote(whole, whole, z_send.at[0, hs], b_recv.at[0], dev(h, p)).wait_send()

        @pl.when((hs >= h) & (h > 0))
        def _():
            remote(whole, whole, z_send.at[1, hs], b_recv.at[0], dev(h, p)).wait_send()

        each_plane(lambda k, q: u_copy(hs, k, q).wait_send())
        each_plane(lambda k, q: u_wait(hs, q))
        return carry

    lax.fori_loop(0, line, drain, 0)
    each_plane(lambda k, q: remote(
        c_out.at[q], c_out.at[q], c_send.at[0], c_recv.at[q], dev(h, p)).wait_recv())


def per_device(row_devices, col_devices, ancestor, factor, diag_inv, structure):
    local_rows, count_sib, width = factor.shape
    lows = max(1, min(row_devices, count_sib // (2 * col_devices)))
    line, group = row_devices // lows, lows * col_devices
    per = count_sib // group
    chunk = per * width // line
    first_row = (lax.axis_index("row") * col_devices + lax.axis_index("col")) * local_rows
    block_ids = (first_row + jnp.arange(local_rows, dtype=jnp.int32)) // RB
    matches = block_ids[:, None, None] == structure[None, :, :]
    row_mask = jnp.any(matches, axis=2).astype(jnp.float32)
    masked = factor * row_mask[:, :, None]
    sent = jnp.transpose(masked.reshape(local_rows, group, per * width), (1, 0, 2))
    dma = pltpu.SemaphoreType.DMA
    vmem = pl.BlockSpec(memory_space=pltpu.VMEM)
    f32 = jnp.float32
    product, update = pl.pallas_call(
        functools.partial(kernel, line, group, lows, col_devices),
        out_shape=(
            jax.ShapeDtypeStruct((group, local_rows, per * width), f32),
            jax.ShapeDtypeStruct((count_sib * width, width), f32),
        ),
        in_specs=[vmem, vmem],
        out_specs=(vmem, vmem),
        scratch_shapes=[
            pltpu.VMEM((group,) + ancestor.shape, f32),
            pltpu.VMEM((line * group * local_rows, per * width), f32),
            pltpu.VMEM((group * local_rows, per * width), f32),
            pltpu.VMEM((per * width, width), f32),
            pltpu.VMEM((line, chunk, width), f32),
            dma((2,)), dma((group,)), dma((group,)), dma((group,)), dma((line * group,)),
            dma((2, line)), dma((group,)), dma((group,)), dma((line,)), dma((line,)),
            dma((line,)), dma((line, group)), dma((line * group,)),
        ],
        compiler_params=pltpu.CompilerParams(collective_id=0, has_side_effects=True),
    )(ancestor, sent)
    product = jnp.transpose(product, (1, 0, 2)).reshape(local_rows, count_sib, width)
    panel = -product * row_mask[:, :, None]
    return panel, diag_inv + update.reshape(count_sib, width, width)


def solution(mesh):
    placed = (P("row", "col"), P(("row", "col"), None, None), P(), P())
    return jax.shard_map(
        functools.partial(per_device, mesh.shape["row"], mesh.shape["col"]),
        mesh=mesh,
        in_specs=placed,
        out_specs=(P(("row", "col"), None, None), P()),
        check_vma=False,
    )
```

```python
import functools

import jax
import jax.numpy as jnp
from jax import lax
from jax.experimental import pallas as pl
from jax.experimental.pallas import tpu as pltpu
from jax.sharding import PartitionSpec as P

RB = 8
CORES = 2
MESH = pl.DeviceIdType.MESH
HIGHEST = lax.Precision.HIGHEST


def kernel(
    line, group, lows, cols,
    a_ref, f_ref, structure_ref, panel_ref, u_out,
    x_buf, mask_buf, m_ref, c_out, a_full, b_buf, c_buf, u_part, u_recv,
    local_sem, a_send, a_recv, b_send, b_recv, z_send,
    c_send, c_recv, r_send, r_recv, l_send, u_send, n_send, u_recv_sem,
):
    row, col = lax.axis_index("row"), lax.axis_index("col")
    h, p = row // lows, (row % lows) * cols + col
    rows, width = m_ref.shape[1], m_ref.shape[2]
    slab = group * rows
    chunk = u_recv.shape[1]
    sib_width = u_part.shape[1]
    per = width // sib_width
    me = h * group + p

    def dev(hq, pq):
        return (hq * lows + pq // cols, pq % cols)

    def remote(src, dst, send, recv, target):
        return pltpu.make_async_remote_copy(
            src_ref=src, dst_ref=dst, send_sem=send, recv_sem=recv,
            device_id=target, device_id_type=MESH,
        )

    def peer(k, n, own):
        return lax.rem(own + k, n)

    def each_plane(body):
        def step(k, carry):
            body(k, peer(k, group, p))
            return carry
        lax.fori_loop(1, group, step, 0)

    def each_line(body):
        def step(k, carry):
            @pl.when(h >= k)
            def _():
                body(h - k)

            @pl.when(h + k < line)
            def _():
                body(h + k)
            return carry
        lax.fori_loop(1, line, step, 0)

    places = group // CORES

    def each_chip(body):
        def step(k, carry):
            body(k, lax.rem(p + k * CORES, group))
            return carry
        lax.fori_loop(1, places, step, 0)

    mate = p + 1 - 2 * lax.rem(p, CORES)

    barrier = pltpu.get_barrier_semaphore()
    each_plane(lambda k, q: pl.semaphore_signal(
        barrier, inc=1, device_id=dev(h, q), device_id_type=MESH))
    each_line(lambda hq: pl.semaphore_signal(
        barrier, inc=1, device_id=dev(hq, p), device_id_type=MESH))

    first_block = me * rows // RB
    for b in range(rows // RB):
        hit = jnp.where(structure_ref[...] == first_block + b, 1.0, 0.0)
        mask = jnp.broadcast_to(jnp.max(hit, axis=1, keepdims=True), mask_buf.shape[1:])
        mask_buf[b] = mask
        x_buf[b * RB:(b + 1) * RB] = f_ref[b * RB:(b + 1) * RB] * mask[None]
    for q in range(group):
        for s in range(per):
            m_ref[q, :, s * sib_width:(s + 1) * sib_width] = x_buf[:, q * per + s, :]
    pl.semaphore_wait(barrier, group + line - 2)

    def piece(hs, q):
        return b_buf.at[pl.ds(pl.multiple_of((hs * group + q) * rows, rows), rows)]

    def b_copy(k, q):
        return remote(m_ref.at[q], piece(h, p), b_send.at[k], b_recv.at[me], dev(h, q))

    def b_wait(hs, q):
        remote(piece(hs, q), piece(hs, q), b_send.at[0], b_recv.at[hs * group + q],
               dev(h, p)).wait_recv()

    def forward(hs, q, to_right):
        side = 0 if to_right else 1
        target = dev(h + 1, p) if to_right else dev(h - 1, p)
        remote(piece(hs, q), piece(hs, q), z_send.at[side, hs],
               b_recv.at[hs * group + q], target).start()

    def a_copy(k, q):
        return remote(a_ref, a_full.at[p], a_send.at[k], a_recv.at[p], dev(h, q))

    own_a = pltpu.make_async_copy(a_ref, a_full.at[p], local_sem.at[0])
    own_b = pltpu.make_async_copy(m_ref.at[p], piece(h, p), local_sem.at[1])
    own_b.start()
    each_plane(lambda k, q: b_copy(k, q).start())
    own_a.start()
    own_b.wait()

    def first(k, carry):
        q = lax.rem(p + group - k, group)

        @pl.when(k > 0)
        def _():
            b_wait(h, q)

        @pl.when(h + 1 < line)
        def _():
            forward(h, q, True)

        @pl.when(h > 0)
        def _():
            forward(h, q, False)

        @pl.when(k == 0)
        def _():
            each_plane(lambda j, r: a_copy(j, r).start())
        return carry

    lax.fori_loop(0, group, first, 0)

    def relay(t, carry):
        def one(k, inner):
            q = lax.rem(p + group - k, group)

            @pl.when(h >= t)
            def _():
                b_wait(h - t, q)

                @pl.when(h + 1 < line)
                def _():
                    forward(h - t, q, True)

            @pl.when(h + t < line)
            def _():
                b_wait(h + t, q)

                @pl.when(h > 0)
                def _():
                    forward(h + t, q, False)
            return inner
        lax.fori_loop(0, group, one, 0)
        return carry

    lax.fori_loop(1, line - 1, relay, 0)

    c_buf[...] = jnp.zeros_like(c_buf)
    own_a.wait()
    each_plane(lambda k, q: remote(
        a_full.at[q], a_full.at[q], a_send.at[0], a_recv.at[q], dev(h, p)).wait_recv())
    a_rows, depth = a_ref.shape
    step = min(slab, depth)

    def multiply(hs):
        for part in range(slab // step):
            start = hs * slab + part * step
            block = b_buf[pl.ds(pl.multiple_of(start, step), step), :]
            at, off = start // depth, start % depth
            for lo in range(lows):
                if step == depth:
                    left = a_full[lo * cols + at]
                else:
                    left = a_full[lo * cols + at, :, pl.ds(pl.multiple_of(off, step), step)]
                c_buf[lo * a_rows:(lo + 1) * a_rows, :] += jnp.dot(
                    left, block, precision=HIGHEST, preferred_element_type=jnp.float32
                )

    def arrived(hs, carry):
        @pl.when((hs - h < line - 1) & (h - hs < line - 1))
        def _():
            multiply(hs)
        return carry

    lax.fori_loop(0, line, arrived, 0)
    last = line - 1

    @pl.when((h == 0) | (h == last))
    def _():
        far = last - h

        def wait_far(k, carry):
            b_wait(far, lax.rem(p + group - k, group))
            return carry

        lax.fori_loop(0, group, wait_far, 0)
        multiply(far)

    mine = pl.ds(pl.multiple_of(h * slab, slab), slab)
    for s in range(per):
        lanes = slice(s * sib_width, (s + 1) * sib_width)
        u_part[s * sib_width:(s + 1) * sib_width, :] = lax.dot_general(
            b_buf[mine, lanes], c_buf[:, lanes], (((0,), (0,)), ((), ())),
            precision=HIGHEST, preferred_element_type=jnp.float32,
        )

    def r_copy(hq):
        return remote(u_part.at[pl.ds(pl.multiple_of(hq * chunk, chunk), chunk)],
                      u_recv.at[h], r_send.at[hq], r_recv.at[h], dev(hq, p))

    def c_copy(k, q):
        return remote(c_buf.at[pl.ds(pl.multiple_of(q * rows, rows), rows)], c_out.at[p],
                      c_send.at[k], c_recv.at[p], dev(h, q))

    each_line(lambda hq: r_copy(hq).start())
    each_plane(lambda k, q: c_copy(k, q).start())
    c_out[p] = c_buf[pl.ds(pl.multiple_of(p * rows, rows), rows), :]
    u_recv[h] = u_part[pl.ds(pl.multiple_of(h * chunk, chunk), chunk), :]
    each_line(lambda hq: remote(
        u_recv.at[hq], u_recv.at[hq], r_send.at[0], r_recv.at[hq], dev(h, p)).wait_recv())
    total = u_recv[0]
    for hs in range(1, line):
        total = total + u_recv[hs]

    def u_at(hs, q):
        return pl.ds(pl.multiple_of((q * line + hs) * chunk, chunk), chunk)

    u_out[u_at(h, p), :] = total

    def l_copy(hq):
        here = u_out.at[u_at(h, p)]
        return remote(here, here, l_send.at[hq], u_recv_sem.at[me], dev(hq, p))

    def u_copy(hs, k, q):
        here = u_out.at[u_at(hs, p)]
        return remote(here, here, u_send.at[hs, k], u_recv_sem.at[hs * group + p], dev(h, q))

    def n_copy(hs, k, q):
        here = u_out.at[u_at(hs, q)]
        return remote(here, here, n_send.at[hs, k], u_recv_sem.at[hs * group + q], dev(h, mate))

    def u_wait(hs, q):
        here = u_out.at[u_at(hs, q)]
        remote(here, here, l_send.at[0], u_recv_sem.at[hs * group + q], dev(h, p)).wait_recv()

    each_line(lambda hq: l_copy(hq).start())

    def spread(hs):
        each_chip(lambda k, q: u_copy(hs, k, q).start())
        n_copy(hs, 0, p).start()

    spread(h)

    def pass_on(hq):
        u_wait(hq, p)
        spread(hq)

    each_line(pass_on)

    each_plane(lambda k, q: remote(
        c_out.at[q], c_out.at[q], c_send.at[0], c_recv.at[q], dev(h, p)).wait_recv())
    for q in range(group):
        for s in range(per):
            x_buf[:, q * per + s, :] = c_out[q, :, s * sib_width:(s + 1) * sib_width]
    for b in range(rows // RB):
        panel_ref[b * RB:(b + 1) * RB] = -x_buf[b * RB:(b + 1) * RB] * mask_buf[b][None]

    def hand_over(hs):
        def one(k, q):
            u_wait(hs, q)
            n_copy(hs, k, q).start()
        each_chip(one)

    hand_over(h)
    each_line(hand_over)

    each_plane(lambda k, q: b_copy(k, q).wait_send())
    each_plane(lambda k, q: a_copy(k, q).wait_send())
    each_plane(lambda k, q: c_copy(k, q).wait_send())
    each_line(lambda hq: r_copy(hq).wait_send())
    each_line(lambda hq: l_copy(hq).wait_send())

    def drain(hs, carry):
        whole = b_buf.at[pl.ds(pl.multiple_of(hs * slab, slab), slab)]

        @pl.when((hs <= h) & (h + 1 < line))
        def _():
            remote(whole, whole, z_send.at[0, hs], b_recv.at[0], dev(h, p)).wait_send()

        @pl.when((hs >= h) & (h > 0))
        def _():
            remote(whole, whole, z_send.at[1, hs], b_recv.at[0], dev(h, p)).wait_send()

        n_copy(hs, 0, p).wait_send()
        each_chip(lambda k, q: u_copy(hs, k, q).wait_send())
        each_chip(lambda k, q: n_copy(hs, k, q).wait_send())
        u_wait(hs, mate)
        each_chip(lambda k, q: u_wait(hs, q + mate - p))
        return carry

    lax.fori_loop(0, line, drain, 0)


def per_device(row_devices, col_devices, ancestor, factor, diag_inv, structure):
    local_rows, count_sib, width = factor.shape
    lows = max(1, min(row_devices, count_sib // (2 * col_devices)))
    line, group = row_devices // lows, lows * col_devices
    per = count_sib // group
    chunk = per * width // line
    dma = pltpu.SemaphoreType.DMA
    vmem = pl.BlockSpec(memory_space=pltpu.VMEM)
    f32 = jnp.float32
    panel, update = pl.pallas_call(
        functools.partial(kernel, line, group, lows, col_devices),
        out_shape=(
            jax.ShapeDtypeStruct(factor.shape, f32),
            jax.ShapeDtypeStruct((count_sib * width, width), f32),
        ),
        in_specs=[vmem, vmem, vmem],
        out_specs=(vmem, vmem),
        scratch_shapes=[
            pltpu.VMEM(factor.shape, f32),
            pltpu.VMEM((local_rows // RB, count_sib, width), f32),
            pltpu.VMEM((group, local_rows, per * width), f32),
            pltpu.VMEM((group, local_rows, per * width), f32),
            pltpu.VMEM((group,) + ancestor.shape, f32),
            pltpu.VMEM((line * group * local_rows, per * width), f32),
            pltpu.VMEM((group * local_rows, per * width), f32),
            pltpu.VMEM((per * width, width), f32),
            pltpu.VMEM((line, chunk, width), f32),
            dma((2,)), dma((group,)), dma((group,)), dma((group,)), dma((line * group,)),
            dma((2, line)), dma((group,)), dma((group,)), dma((line,)), dma((line,)),
            dma((line,)), dma((line, group // CORES)), dma((line, group // CORES)), dma((line * group,)),
        ],
        compiler_params=pltpu.CompilerParams(collective_id=0, has_side_effects=True),
    )(ancestor, factor, structure)
    return panel, diag_inv + update.reshape(count_sib, width, width)


def solution(mesh):
    placed = (P("row", "col"), P(("row", "col"), None, None), P(), P())
    return jax.shard_map(
        functools.partial(per_device, mesh.shape["row"], mesh.shape["col"]),
        mesh=mesh,
        in_specs=placed,
        out_specs=(P(("row", "col"), None, None), P()),
        check_vma=False,
    )
```

```python
import functools

import jax
import jax.numpy as jnp
from jax import lax
from jax.experimental import pallas as pl
from jax.experimental.pallas import tpu as pltpu
from jax.sharding import PartitionSpec as P

RB = 8
CORES = 2
MESH = pl.DeviceIdType.MESH
HIGHEST = lax.Precision.HIGHEST


def kernel(
    line, group, lows, cols,
    a_ref, f_ref, structure_ref, diag_ref, panel_ref, u_out,
    d_buf, x_buf, mask_buf, m_ref, c_out, a_full, b_buf, c_buf, u_part, u_recv,
    local_sem, a_send, a_recv, b_send, b_recv, z_send,
    c_send, c_recv, r_send, r_recv, l_send, u_send, n_send, u_recv_sem,
):
    row, col = lax.axis_index("row"), lax.axis_index("col")
    h, p = row // lows, (row % lows) * cols + col
    rows, width = m_ref.shape[1], m_ref.shape[2]
    slab = group * rows
    chunk = u_recv.shape[1]
    sib_width = u_part.shape[1]
    per = width // sib_width
    me = h * group + p

    def dev(hq, pq):
        return (hq * lows + pq // cols, pq % cols)

    def remote(src, dst, send, recv, target):
        return pltpu.make_async_remote_copy(
            src_ref=src, dst_ref=dst, send_sem=send, recv_sem=recv,
            device_id=target, device_id_type=MESH,
        )

    def peer(k, n, own):
        return lax.rem(own + k, n)

    def each_plane(body):
        def step(k, carry):
            body(k, peer(k, group, p))
            return carry
        lax.fori_loop(1, group, step, 0)

    def each_line(body):
        def step(k, carry):
            @pl.when(h >= k)
            def _():
                body(h - k)

            @pl.when(h + k < line)
            def _():
                body(h + k)
            return carry
        lax.fori_loop(1, line, step, 0)

    places = group // CORES

    def each_chip(body):
        def step(k, carry):
            body(k, lax.rem(p + k * CORES, group))
            return carry
        lax.fori_loop(1, places, step, 0)

    mate = p + 1 - 2 * lax.rem(p, CORES)

    def u_at(hs, q):
        return pl.ds(pl.multiple_of((q * line + hs) * chunk, chunk), chunk)

    own_diag = pltpu.make_async_copy(diag_ref.at[u_at(h, p)], d_buf, local_sem.at[2])
    own_diag.start()
    barrier = pltpu.get_barrier_semaphore()
    each_plane(lambda k, q: pl.semaphore_signal(
        barrier, inc=1, device_id=dev(h, q), device_id_type=MESH))
    each_line(lambda hq: pl.semaphore_signal(
        barrier, inc=1, device_id=dev(hq, p), device_id_type=MESH))

    first_block = me * rows // RB
    for b in range(rows // RB):
        hit = jnp.where(structure_ref[...] == first_block + b, 1.0, 0.0)
        mask = jnp.broadcast_to(jnp.max(hit, axis=1, keepdims=True), mask_buf.shape[1:])
        mask_buf[b] = mask
        x_buf[b * RB:(b + 1) * RB] = f_ref[b * RB:(b + 1) * RB] * mask[None]
    for q in range(group):
        for s in range(per):
            m_ref[q, :, s * sib_width:(s + 1) * sib_width] = x_buf[:, q * per + s, :]
    pl.semaphore_wait(barrier, group + line - 2)

    def piece(hs, q):
        return b_buf.at[pl.ds(pl.multiple_of((hs * group + q) * rows, rows), rows)]

    def b_copy(k, q):
        return remote(m_ref.at[q], piece(h, p), b_send.at[k], b_recv.at[me], dev(h, q))

    def b_wait(hs, q):
        remote(piece(hs, q), piece(hs, q), b_send.at[0], b_recv.at[hs * group + q],
               dev(h, p)).wait_recv()

    def forward(hs, q, to_right):
        side = 0 if to_right else 1
        target = dev(h + 1, p) if to_right else dev(h - 1, p)
        remote(piece(hs, q), piece(hs, q), z_send.at[side, hs],
               b_recv.at[hs * group + q], target).start()

    def a_copy(k, q):
        return remote(a_ref, a_full.at[p], a_send.at[k], a_recv.at[p], dev(h, q))

    own_a = pltpu.make_async_copy(a_ref, a_full.at[p], local_sem.at[0])
    own_b = pltpu.make_async_copy(m_ref.at[p], piece(h, p), local_sem.at[1])
    own_b.start()
    each_plane(lambda k, q: b_copy(k, q).start())
    own_a.start()
    own_b.wait()

    def first(k, carry):
        q = lax.rem(p + group - k, group)

        @pl.when(k > 0)
        def _():
            b_wait(h, q)

        @pl.when(h + 1 < line)
        def _():
            forward(h, q, True)

        @pl.when(h > 0)
        def _():
            forward(h, q, False)

        @pl.when(k == 0)
        def _():
            each_plane(lambda j, r: a_copy(j, r).start())
        return carry

    lax.fori_loop(0, group, first, 0)

    def relay(t, carry):
        def one(k, inner):
            q = lax.rem(p + group - k, group)

            @pl.when(h >= t)
            def _():
                b_wait(h - t, q)

                @pl.when(h + 1 < line)
                def _():
                    forward(h - t, q, True)

            @pl.when(h + t < line)
            def _():
                b_wait(h + t, q)

                @pl.when(h > 0)
                def _():
                    forward(h + t, q, False)
            return inner
        lax.fori_loop(0, group, one, 0)
        return carry

    lax.fori_loop(1, line - 1, relay, 0)

    c_buf[...] = jnp.zeros_like(c_buf)
    own_a.wait()
    each_plane(lambda k, q: remote(
        a_full.at[q], a_full.at[q], a_send.at[0], a_recv.at[q], dev(h, p)).wait_recv())
    a_rows, depth = a_ref.shape
    step = min(slab, depth)

    def multiply(hs):
        for part in range(slab // step):
            start = hs * slab + part * step
            block = b_buf[pl.ds(pl.multiple_of(start, step), step), :]
            at, off = start // depth, start % depth
            for lo in range(lows):
                if step == depth:
                    left = a_full[lo * cols + at]
                else:
                    left = a_full[lo * cols + at, :, pl.ds(pl.multiple_of(off, step), step)]
                c_buf[lo * a_rows:(lo + 1) * a_rows, :] += jnp.dot(
                    left, block, precision=HIGHEST, preferred_element_type=jnp.float32
                )

    def arrived(hs, carry):
        @pl.when((hs - h < line - 1) & (h - hs < line - 1))
        def _():
            multiply(hs)
        return carry

    lax.fori_loop(0, line, arrived, 0)
    last = line - 1

    @pl.when((h == 0) | (h == last))
    def _():
        far = last - h

        def wait_far(k, carry):
            b_wait(far, lax.rem(p + group - k, group))
            return carry

        lax.fori_loop(0, group, wait_far, 0)
        multiply(far)

    mine = pl.ds(pl.multiple_of(h * slab, slab), slab)
    for s in range(per):
        lanes = slice(s * sib_width, (s + 1) * sib_width)
        u_part[s * sib_width:(s + 1) * sib_width, :] = lax.dot_general(
            b_buf[mine, lanes], c_buf[:, lanes], (((0,), (0,)), ((), ())),
            precision=HIGHEST, preferred_element_type=jnp.float32,
        )

    def r_copy(hq):
        return remote(u_part.at[pl.ds(pl.multiple_of(hq * chunk, chunk), chunk)],
                      u_recv.at[h], r_send.at[hq], r_recv.at[h], dev(hq, p))

    def c_copy(k, q):
        return remote(c_buf.at[pl.ds(pl.multiple_of(q * rows, rows), rows)], c_out.at[p],
                      c_send.at[k], c_recv.at[p], dev(h, q))

    each_line(lambda hq: r_copy(hq).start())
    each_plane(lambda k, q: c_copy(k, q).start())
    c_out[p] = c_buf[pl.ds(pl.multiple_of(p * rows, rows), rows), :]
    u_recv[h] = u_part[pl.ds(pl.multiple_of(h * chunk, chunk), chunk), :]
    each_line(lambda hq: remote(
        u_recv.at[hq], u_recv.at[hq], r_send.at[0], r_recv.at[hq], dev(h, p)).wait_recv())
    total = u_recv[0]
    for hs in range(1, line):
        total = total + u_recv[hs]

    own_diag.wait()
    u_out[u_at(h, p), :] = d_buf[...] + total

    def l_copy(hq):
        here = u_out.at[u_at(h, p)]
        return remote(here, here, l_send.at[hq], u_recv_sem.at[me], dev(hq, p))

    def u_copy(hs, k, q):
        here = u_out.at[u_at(hs, p)]
        return remote(here, here, u_send.at[hs, k], u_recv_sem.at[hs * group + p], dev(h, q))

    def n_copy(hs, k, q):
        here = u_out.at[u_at(hs, q)]
        return remote(here, here, n_send.at[hs, k], u_recv_sem.at[hs * group + q], dev(h, mate))

    def u_wait(hs, q):
        here = u_out.at[u_at(hs, q)]
        remote(here, here, l_send.at[0], u_recv_sem.at[hs * group + q], dev(h, p)).wait_recv()

    each_line(lambda hq: l_copy(hq).start())

    def spread(hs):
        each_chip(lambda k, q: u_copy(hs, k, q).start())
        n_copy(hs, 0, p).start()

    spread(h)

    def pass_on(hq):
        u_wait(hq, p)
        spread(hq)

    each_line(pass_on)

    each_plane(lambda k, q: remote(
        c_out.at[q], c_out.at[q], c_send.at[0], c_recv.at[q], dev(h, p)).wait_recv())
    for q in range(group):
        for s in range(per):
            x_buf[:, q * per + s, :] = c_out[q, :, s * sib_width:(s + 1) * sib_width]
    for b in range(rows // RB):
        panel_ref[b * RB:(b + 1) * RB] = -x_buf[b * RB:(b + 1) * RB] * mask_buf[b][None]

    def hand_over(hs):
        def one(k, q):
            u_wait(hs, q)
            n_copy(hs, k, q).start()
        each_chip(one)

    hand_over(h)
    each_line(hand_over)

    each_plane(lambda k, q: b_copy(k, q).wait_send())
    each_plane(lambda k, q: a_copy(k, q).wait_send())
    each_plane(lambda k, q: c_copy(k, q).wait_send())
    each_line(lambda hq: r_copy(hq).wait_send())
    each_line(lambda hq: l_copy(hq).wait_send())

    def drain(hs, carry):
        whole = b_buf.at[pl.ds(pl.multiple_of(hs * slab, slab), slab)]

        @pl.when((hs <= h) & (h + 1 < line))
        def _():
            remote(whole, whole, z_send.at[0, hs], b_recv.at[0], dev(h, p)).wait_send()

        @pl.when((hs >= h) & (h > 0))
        def _():
            remote(whole, whole, z_send.at[1, hs], b_recv.at[0], dev(h, p)).wait_send()

        n_copy(hs, 0, p).wait_send()
        each_chip(lambda k, q: u_copy(hs, k, q).wait_send())
        each_chip(lambda k, q: n_copy(hs, k, q).wait_send())
        u_wait(hs, mate)
        each_chip(lambda k, q: u_wait(hs, q + mate - p))
        return carry

    lax.fori_loop(0, line, drain, 0)


def per_device(row_devices, col_devices, ancestor, factor, diag_inv, structure):
    local_rows, count_sib, width = factor.shape
    lows = max(1, min(row_devices, count_sib // (2 * col_devices)))
    line, group = row_devices // lows, lows * col_devices
    per = count_sib // group
    chunk = per * width // line
    dma = pltpu.SemaphoreType.DMA
    vmem = pl.BlockSpec(memory_space=pltpu.VMEM)
    f32 = jnp.float32
    panel, update = pl.pallas_call(
        functools.partial(kernel, line, group, lows, col_devices),
        out_shape=(
            pltpu.VMEM(factor.shape, f32),
            pltpu.VMEM((count_sib * width, width), f32),
        ),
        in_specs=[vmem, vmem, vmem, pl.BlockSpec(memory_space=pl.ANY)],
        out_specs=(vmem, vmem),
        scratch_shapes=[
            pltpu.VMEM((chunk, width), f32),
            pltpu.VMEM(factor.shape, f32),
            pltpu.VMEM((local_rows // RB, count_sib, width), f32),
            pltpu.VMEM((group, local_rows, per * width), f32),
            pltpu.VMEM((group, local_rows, per * width), f32),
            pltpu.VMEM((group,) + ancestor.shape, f32),
            pltpu.VMEM((line * group * local_rows, per * width), f32),
            pltpu.VMEM((group * local_rows, per * width), f32),
            pltpu.VMEM((per * width, width), f32),
            pltpu.VMEM((line, chunk, width), f32),
            dma((3,)), dma((group,)), dma((group,)), dma((group,)), dma((line * group,)),
            dma((2, line)), dma((group,)), dma((group,)), dma((line,)), dma((line,)),
            dma((line,)), dma((line, group // CORES)), dma((line, group // CORES)), dma((line * group,)),
        ],
        compiler_params=pltpu.CompilerParams(collective_id=0, has_side_effects=True),
    )(ancestor, factor, structure, diag_inv.reshape(count_sib * width, width))
    return panel, update.reshape(count_sib, width, width)


def solution(mesh):
    placed = (P("row", "col"), P(("row", "col"), None, None), P(), P())
    return jax.shard_map(
        functools.partial(per_device, mesh.shape["row"], mesh.shape["col"]),
        mesh=mesh,
        in_specs=placed,
        out_specs=(P(("row", "col"), None, None), P()),
        check_vma=False,
    )
```

```python
import functools

import jax
import jax.numpy as jnp
from jax import lax
from jax.experimental import pallas as pl
from jax.experimental.pallas import tpu as pltpu
from jax.sharding import PartitionSpec as P

RB = 8
CORES = 2
MESH = pl.DeviceIdType.MESH
HIGHEST = lax.Precision.HIGHEST


def kernel(
    line, group, lows, cols,
    a_in, f_in, structure_in, diag_ref, panel_ref, u_out,
    f_ref, structure_ref, d_buf, x_buf, mask_buf, m_ref, c_out, a_full, b_buf, c_buf, u_part, u_recv,
    local_sem, a_send, a_recv, b_send, b_recv, z_send,
    c_send, c_recv, r_send, r_recv, l_send, u_send, n_send, u_recv_sem,
):
    row, col = lax.axis_index("row"), lax.axis_index("col")
    h, p = row // lows, (row % lows) * cols + col
    rows, width = m_ref.shape[1], m_ref.shape[2]
    slab = group * rows
    chunk = u_recv.shape[1]
    sib_width = u_part.shape[1]
    per = width // sib_width
    me = h * group + p

    def dev(hq, pq):
        return (hq * lows + pq // cols, pq % cols)

    def remote(src, dst, send, recv, target):
        return pltpu.make_async_remote_copy(
            src_ref=src, dst_ref=dst, send_sem=send, recv_sem=recv,
            device_id=target, device_id_type=MESH,
        )

    def peer(k, n, own):
        return lax.rem(own + k, n)

    def each_plane(body):
        def step(k, carry):
            body(k, peer(k, group, p))
            return carry
        lax.fori_loop(1, group, step, 0)

    def each_line(body):
        def step(k, carry):
            @pl.when(h >= k)
            def _():
                body(h - k)

            @pl.when(h + k < line)
            def _():
                body(h + k)
            return carry
        lax.fori_loop(1, line, step, 0)

    places = group // CORES

    def each_chip(body):
        def step(k, carry):
            body(k, lax.rem(p + k * CORES, group))
            return carry
        lax.fori_loop(1, places, step, 0)

    mate = p + 1 - 2 * lax.rem(p, CORES)

    def u_at(hs, q):
        return pl.ds(pl.multiple_of((q * line + hs) * chunk, chunk), chunk)

    own_diag = pltpu.make_async_copy(diag_ref.at[u_at(h, p)], d_buf, local_sem.at[2])
    own_diag.start()
    own_f = pltpu.make_async_copy(f_in, f_ref, local_sem.at[3])
    own_f.start()
    own_structure = pltpu.make_async_copy(structure_in, structure_ref, local_sem.at[4])
    own_structure.start()
    own_a = pltpu.make_async_copy(a_in, a_full.at[p], local_sem.at[0])
    own_a.start()
    barrier = pltpu.get_barrier_semaphore()
    each_plane(lambda k, q: pl.semaphore_signal(
        barrier, inc=1, device_id=dev(h, q), device_id_type=MESH))
    each_line(lambda hq: pl.semaphore_signal(
        barrier, inc=1, device_id=dev(hq, p), device_id_type=MESH))

    own_structure.wait()
    own_f.wait()
    first_block = me * rows // RB
    for b in range(rows // RB):
        hit = jnp.where(structure_ref[...] == first_block + b, 1.0, 0.0)
        mask = jnp.broadcast_to(jnp.max(hit, axis=1, keepdims=True), mask_buf.shape[1:])
        mask_buf[b] = mask
        x_buf[b * RB:(b + 1) * RB] = f_ref[b * RB:(b + 1) * RB] * mask[None]
    for q in range(group):
        for s in range(per):
            m_ref[q, :, s * sib_width:(s + 1) * sib_width] = x_buf[:, q * per + s, :]
    pl.semaphore_wait(barrier, group + line - 2)

    def piece(hs, q):
        return b_buf.at[pl.ds(pl.multiple_of((hs * group + q) * rows, rows), rows)]

    def b_copy(k, q):
        return remote(m_ref.at[q], piece(h, p), b_send.at[k], b_recv.at[me], dev(h, q))

    def b_wait(hs, q):
        remote(piece(hs, q), piece(hs, q), b_send.at[0], b_recv.at[hs * group + q],
               dev(h, p)).wait_recv()

    def forward(hs, q, to_right):
        side = 0 if to_right else 1
        target = dev(h + 1, p) if to_right else dev(h - 1, p)
        remote(piece(hs, q), piece(hs, q), z_send.at[side, hs],
               b_recv.at[hs * group + q], target).start()

    def a_copy(k, q):
        return remote(a_full.at[p], a_full.at[p], a_send.at[k], a_recv.at[p], dev(h, q))

    own_b = pltpu.make_async_copy(m_ref.at[p], piece(h, p), local_sem.at[1])
    own_b.start()
    each_plane(lambda k, q: b_copy(k, q).start())
    own_a.wait()
    own_b.wait()

    def first(k, carry):
        q = lax.rem(p + group - k, group)

        @pl.when(k > 0)
        def _():
            b_wait(h, q)

        @pl.when(h + 1 < line)
        def _():
            forward(h, q, True)

        @pl.when(h > 0)
        def _():
            forward(h, q, False)

        @pl.when(k == 0)
        def _():
            each_plane(lambda j, r: a_copy(j, r).start())
        return carry

    lax.fori_loop(0, group, first, 0)

    def relay(t, carry):
        def one(k, inner):
            q = lax.rem(p + group - k, group)

            @pl.when(h >= t)
            def _():
                b_wait(h - t, q)

                @pl.when(h + 1 < line)
                def _():
                    forward(h - t, q, True)

            @pl.when(h + t < line)
            def _():
                b_wait(h + t, q)

                @pl.when(h > 0)
                def _():
                    forward(h + t, q, False)
            return inner
        lax.fori_loop(0, group, one, 0)
        return carry

    lax.fori_loop(1, line - 1, relay, 0)

    c_buf[...] = jnp.zeros_like(c_buf)
    each_plane(lambda k, q: remote(
        a_full.at[q], a_full.at[q], a_send.at[0], a_recv.at[q], dev(h, p)).wait_recv())
    a_rows, depth = a_in.shape
    step = min(slab, depth)

    def multiply(hs):
        for part in range(slab // step):
            start = hs * slab + part * step
            block = b_buf[pl.ds(pl.multiple_of(start, step), step), :]
            at, off = start // depth, start % depth
            for lo in range(lows):
                if step == depth:
                    left = a_full[lo * cols + at]
                else:
                    left = a_full[lo * cols + at, :, pl.ds(pl.multiple_of(off, step), step)]
                c_buf[lo * a_rows:(lo + 1) * a_rows, :] += jnp.dot(
                    left, block, precision=HIGHEST, preferred_element_type=jnp.float32
                )

    def arrived(hs, carry):
        @pl.when((hs - h < line - 1) & (h - hs < line - 1))
        def _():
            multiply(hs)
        return carry

    lax.fori_loop(0, line, arrived, 0)
    last = line - 1

    @pl.when((h == 0) | (h == last))
    def _():
        far = last - h

        def wait_far(k, carry):
            b_wait(far, lax.rem(p + group - k, group))
            return carry

        lax.fori_loop(0, group, wait_far, 0)
        multiply(far)

    mine = pl.ds(pl.multiple_of(h * slab, slab), slab)
    for s in range(per):
        lanes = slice(s * sib_width, (s + 1) * sib_width)
        u_part[s * sib_width:(s + 1) * sib_width, :] = lax.dot_general(
            b_buf[mine, lanes], c_buf[:, lanes], (((0,), (0,)), ((), ())),
            precision=HIGHEST, preferred_element_type=jnp.float32,
        )

    def r_copy(hq):
        return remote(u_part.at[pl.ds(pl.multiple_of(hq * chunk, chunk), chunk)],
                      u_recv.at[h], r_send.at[hq], r_recv.at[h], dev(hq, p))

    def c_copy(k, q):
        return remote(c_buf.at[pl.ds(pl.multiple_of(q * rows, rows), rows)], c_out.at[p],
                      c_send.at[k], c_recv.at[p], dev(h, q))

    each_line(lambda hq: r_copy(hq).start())
    each_plane(lambda k, q: c_copy(k, q).start())
    c_out[p] = c_buf[pl.ds(pl.multiple_of(p * rows, rows), rows), :]
    u_recv[h] = u_part[pl.ds(pl.multiple_of(h * chunk, chunk), chunk), :]
    each_line(lambda hq: remote(
        u_recv.at[hq], u_recv.at[hq], r_send.at[0], r_recv.at[hq], dev(h, p)).wait_recv())
    total = u_recv[0]
    for hs in range(1, line):
        total = total + u_recv[hs]

    own_diag.wait()
    u_out[u_at(h, p), :] = d_buf[...] + total

    def l_copy(hq):
        here = u_out.at[u_at(h, p)]
        return remote(here, here, l_send.at[hq], u_recv_sem.at[me], dev(hq, p))

    def u_copy(hs, k, q):
        here = u_out.at[u_at(hs, p)]
        return remote(here, here, u_send.at[hs, k], u_recv_sem.at[hs * group + p], dev(h, q))

    def n_copy(hs, k, q):
        here = u_out.at[u_at(hs, q)]
        return remote(here, here, n_send.at[hs, k], u_recv_sem.at[hs * group + q], dev(h, mate))

    def u_wait(hs, q):
        here = u_out.at[u_at(hs, q)]
        remote(here, here, l_send.at[0], u_recv_sem.at[hs * group + q], dev(h, p)).wait_recv()

    each_line(lambda hq: l_copy(hq).start())

    def spread(hs):
        each_chip(lambda k, q: u_copy(hs, k, q).start())
        n_copy(hs, 0, p).start()

    spread(h)

    def pass_on(hq):
        u_wait(hq, p)
        spread(hq)

    each_line(pass_on)

    each_plane(lambda k, q: remote(
        c_out.at[q], c_out.at[q], c_send.at[0], c_recv.at[q], dev(h, p)).wait_recv())
    for q in range(group):
        for s in range(per):
            x_buf[:, q * per + s, :] = c_out[q, :, s * sib_width:(s + 1) * sib_width]
    for b in range(rows // RB):
        panel_ref[b * RB:(b + 1) * RB] = -x_buf[b * RB:(b + 1) * RB] * mask_buf[b][None]

    def hand_over(hs):
        def one(k, q):
            u_wait(hs, q)
            n_copy(hs, k, q).start()
        each_chip(one)

    hand_over(h)
    each_line(hand_over)

    each_plane(lambda k, q: b_copy(k, q).wait_send())
    each_plane(lambda k, q: a_copy(k, q).wait_send())
    each_plane(lambda k, q: c_copy(k, q).wait_send())
    each_line(lambda hq: r_copy(hq).wait_send())
    each_line(lambda hq: l_copy(hq).wait_send())

    def drain(hs, carry):
        whole = b_buf.at[pl.ds(pl.multiple_of(hs * slab, slab), slab)]

        @pl.when((hs <= h) & (h + 1 < line))
        def _():
            remote(whole, whole, z_send.at[0, hs], b_recv.at[0], dev(h, p)).wait_send()

        @pl.when((hs >= h) & (h > 0))
        def _():
            remote(whole, whole, z_send.at[1, hs], b_recv.at[0], dev(h, p)).wait_send()

        n_copy(hs, 0, p).wait_send()
        each_chip(lambda k, q: u_copy(hs, k, q).wait_send())
        each_chip(lambda k, q: n_copy(hs, k, q).wait_send())
        u_wait(hs, mate)
        each_chip(lambda k, q: u_wait(hs, q + mate - p))
        return carry

    lax.fori_loop(0, line, drain, 0)


def leave(panel_in, update_in, panel_out, update_out, sem):
    first = pltpu.make_async_copy(update_in, update_out, sem.at[0])
    second = pltpu.make_async_copy(panel_in, panel_out, sem.at[1])
    first.start()
    second.start()
    first.wait()
    second.wait()


def per_device(row_devices, col_devices, ancestor, factor, diag_inv, structure):
    local_rows, count_sib, width = factor.shape
    lows = max(1, min(row_devices, count_sib // (2 * col_devices)))
    line, group = row_devices // lows, lows * col_devices
    per = count_sib // group
    chunk = per * width // line
    dma = pltpu.SemaphoreType.DMA
    vmem = pl.BlockSpec(memory_space=pltpu.VMEM)
    anywhere = pl.BlockSpec(memory_space=pl.ANY)
    f32 = jnp.float32
    panel, update = pl.pallas_call(
        functools.partial(kernel, line, group, lows, col_devices),
        out_shape=(
            pltpu.VMEM(factor.shape, f32),
            pltpu.VMEM((count_sib * width, width), f32),
        ),
        in_specs=[anywhere] * 4,
        out_specs=(vmem, vmem),
        scratch_shapes=[
            pltpu.VMEM(factor.shape, f32),
            pltpu.VMEM(structure.shape, structure.dtype),
            pltpu.VMEM((chunk, width), f32),
            pltpu.VMEM(factor.shape, f32),
            pltpu.VMEM((local_rows // RB, count_sib, width), f32),
            pltpu.VMEM((group, local_rows, per * width), f32),
            pltpu.VMEM((group, local_rows, per * width), f32),
            pltpu.VMEM((group,) + ancestor.shape, f32),
            pltpu.VMEM((line * group * local_rows, per * width), f32),
            pltpu.VMEM((group * local_rows, per * width), f32),
            pltpu.VMEM((per * width, width), f32),
            pltpu.VMEM((line, chunk, width), f32),
            dma((5,)), dma((group,)), dma((group,)), dma((group,)), dma((line * group,)),
            dma((2, line)), dma((group,)), dma((group,)), dma((line,)), dma((line,)),
            dma((line,)), dma((line, group // CORES)), dma((line, group // CORES)), dma((line * group,)),
        ],
        compiler_params=pltpu.CompilerParams(collective_id=0, has_side_effects=True),
    )(ancestor, factor, structure, diag_inv.reshape(count_sib * width, width))
    panel, update = pl.pallas_call(
        leave,
        out_shape=(
            jax.ShapeDtypeStruct(panel.shape, f32), jax.ShapeDtypeStruct(update.shape, f32),
        ),
        in_specs=[vmem] * 2,
        out_specs=(anywhere, anywhere),
        scratch_shapes=[dma((2,))],
    )(pltpu.with_memory_space_constraint(panel, pltpu.VMEM), pltpu.with_memory_space_constraint(update, pltpu.VMEM))
    return panel, update.reshape(count_sib, width, width)


def solution(mesh):
    placed = (P("row", "col"), P(("row", "col"), None, None), P(), P())
    return jax.shard_map(
        functools.partial(per_device, mesh.shape["row"], mesh.shape["col"]),
        mesh=mesh,
        in_specs=placed,
        out_specs=(P(("row", "col"), None, None), P()),
        check_vma=False,
    )
```

```python
import functools

import jax
import jax.numpy as jnp
from jax import lax
from jax.experimental import pallas as pl
from jax.experimental.pallas import tpu as pltpu
from jax.sharding import PartitionSpec as P

RB = 8
CORES = 2
MESH = pl.DeviceIdType.MESH
HIGHEST = lax.Precision.HIGHEST


def kernel(
    line, group, lows, cols,
    a_in, f_in, structure_in, diag_ref, panel_ref, u_out,
    f_ref, structure_ref, d_buf, x_buf, mask_buf, m_ref, c_out, a_full, b_buf, c_buf, u_part, u_recv,
    local_sem, a_send, a_recv, b_send, b_recv, z_send,
    c_send, c_recv, r_send, r_recv, l_send, u_send, n_send, u_recv_sem,
):
    row, col = lax.axis_index("row"), lax.axis_index("col")
    h, p = row // lows, (row % lows) * cols + col
    rows, width = m_ref.shape[1], m_ref.shape[2]
    slab = group * rows
    chunk = u_recv.shape[1]
    sib_width = u_part.shape[1]
    per = width // sib_width
    me = h * group + p

    def dev(hq, pq):
        return (hq * lows + pq // cols, pq % cols)

    def remote(src, dst, send, recv, target):
        return pltpu.make_async_remote_copy(
            src_ref=src, dst_ref=dst, send_sem=send, recv_sem=recv,
            device_id=target, device_id_type=MESH,
        )

    def peer(k, n, own):
        return lax.rem(own + k, n)

    def each_plane(body):
        def step(k, carry):
            body(k, peer(k, group, p))
            return carry
        lax.fori_loop(1, group, step, 0)

    def each_line(body):
        def step(k, carry):
            @pl.when(h >= k)
            def _():
                body(h - k)

            @pl.when(h + k < line)
            def _():
                body(h + k)
            return carry
        lax.fori_loop(1, line, step, 0)

    places = group // CORES

    def each_chip(body):
        def step(k, carry):
            body(k, lax.rem(p + k * CORES, group))
            return carry
        lax.fori_loop(1, places, step, 0)

    mate = p + 1 - 2 * lax.rem(p, CORES)

    def u_at(hs, q):
        return pl.ds(pl.multiple_of((q * line + hs) * chunk, chunk), chunk)

    own_diag = pltpu.make_async_copy(diag_ref.at[u_at(h, p)], d_buf, local_sem.at[2])
    own_diag.start()
    own_f = pltpu.make_async_copy(f_in, f_ref, local_sem.at[3])
    own_f.start()
    own_structure = pltpu.make_async_copy(structure_in, structure_ref, local_sem.at[4])
    own_structure.start()
    own_a = pltpu.make_async_copy(a_in, a_full.at[p], local_sem.at[0])
    own_a.start()
    barrier = pltpu.get_barrier_semaphore()
    each_plane(lambda k, q: pl.semaphore_signal(
        barrier, inc=1, device_id=dev(h, q), device_id_type=MESH))
    each_line(lambda hq: pl.semaphore_signal(
        barrier, inc=1, device_id=dev(hq, p), device_id_type=MESH))

    own_structure.wait()
    own_f.wait()
    first_block = me * rows // RB
    for b in range(rows // RB):
        hit = jnp.where(structure_ref[...] == first_block + b, 1.0, 0.0)
        mask = jnp.broadcast_to(jnp.max(hit, axis=1, keepdims=True), mask_buf.shape[1:])
        mask_buf[b] = mask
        x_buf[b * RB:(b + 1) * RB] = f_ref[b * RB:(b + 1) * RB] * mask[None]
    for q in range(group):
        for s in range(per):
            m_ref[q, :, s * sib_width:(s + 1) * sib_width] = x_buf[:, q * per + s, :]
    pl.semaphore_wait(barrier, group + line - 2)

    def piece(hs, q):
        return b_buf.at[pl.ds(pl.multiple_of((hs * group + q) * rows, rows), rows)]

    def b_copy(k, q):
        return remote(m_ref.at[q], piece(h, p), b_send.at[k], b_recv.at[me], dev(h, q))

    def b_wait(hs, q):
        remote(piece(hs, q), piece(hs, q), b_send.at[0], b_recv.at[hs * group + q],
               dev(h, p)).wait_recv()

    def forward(hs, q, to_right):
        side = 0 if to_right else 1
        target = dev(h + 1, p) if to_right else dev(h - 1, p)
        remote(piece(hs, q), piece(hs, q), z_send.at[side, hs],
               b_recv.at[hs * group + q], target).start()

    def a_copy(k, q):
        return remote(a_full.at[p], a_full.at[p], a_send.at[k], a_recv.at[p], dev(h, q))

    own_b = pltpu.make_async_copy(m_ref.at[p], piece(h, p), local_sem.at[1])
    own_b.start()
    each_plane(lambda k, q: b_copy(k, q).start())
    own_a.wait()
    own_b.wait()

    def first(k, carry):
        q = lax.rem(p + group - k, group)

        @pl.when(k > 0)
        def _():
            b_wait(h, q)

        @pl.when(h + 1 < line)
        def _():
            forward(h, q, True)

        @pl.when(h > 0)
        def _():
            forward(h, q, False)

        return carry

    lax.fori_loop(0, group, first, 0)
    each_plane(lambda k, q: a_copy(k, q).start())

    def relay(t, carry):
        def one(k, inner):
            q = lax.rem(p + group - k, group)

            @pl.when(h >= t)
            def _():
                b_wait(h - t, q)

                @pl.when(h + 1 < line)
                def _():
                    forward(h - t, q, True)

            @pl.when(h + t < line)
            def _():
                b_wait(h + t, q)

                @pl.when(h > 0)
                def _():
                    forward(h + t, q, False)
            return inner
        lax.fori_loop(0, group, one, 0)
        return carry

    lax.fori_loop(1, line - 1, relay, 0)

    c_buf[...] = jnp.zeros_like(c_buf)
    each_plane(lambda k, q: remote(
        a_full.at[q], a_full.at[q], a_send.at[0], a_recv.at[q], dev(h, p)).wait_recv())
    a_rows, depth = a_in.shape
    step = min(slab, depth)

    def multiply(hs):
        for part in range(slab // step):
            start = hs * slab + part * step
            block = b_buf[pl.ds(pl.multiple_of(start, step), step), :]
            at, off = start // depth, start % depth
            for lo in range(lows):
                if step == depth:
                    left = a_full[lo * cols + at]
                else:
                    left = a_full[lo * cols + at, :, pl.ds(pl.multiple_of(off, step), step)]
                c_buf[lo * a_rows:(lo + 1) * a_rows, :] += jnp.dot(
                    left, block, precision=HIGHEST, preferred_element_type=jnp.float32
                )

    def arrived(hs, carry):
        @pl.when((hs - h < line - 1) & (h - hs < line - 1))
        def _():
            multiply(hs)
        return carry

    lax.fori_loop(0, line, arrived, 0)
    last = line - 1

    @pl.when((h == 0) | (h == last))
    def _():
        far = last - h

        def wait_far(k, carry):
            b_wait(far, lax.rem(p + group - k, group))
            return carry

        lax.fori_loop(0, group, wait_far, 0)
        multiply(far)

    mine = pl.ds(pl.multiple_of(h * slab, slab), slab)
    for s in range(per):
        lanes = slice(s * sib_width, (s + 1) * sib_width)
        u_part[s * sib_width:(s + 1) * sib_width, :] = lax.dot_general(
            b_buf[mine, lanes], c_buf[:, lanes], (((0,), (0,)), ((), ())),
            precision=HIGHEST, preferred_element_type=jnp.float32,
        )

    def r_copy(hq):
        return remote(u_part.at[pl.ds(pl.multiple_of(hq * chunk, chunk), chunk)],
                      u_recv.at[h], r_send.at[hq], r_recv.at[h], dev(hq, p))

    def c_copy(k, q):
        return remote(c_buf.at[pl.ds(pl.multiple_of(q * rows, rows), rows)], c_out.at[p],
                      c_send.at[k], c_recv.at[p], dev(h, q))

    each_line(lambda hq: r_copy(hq).start())
    each_plane(lambda k, q: c_copy(k, q).start())
    c_out[p] = c_buf[pl.ds(pl.multiple_of(p * rows, rows), rows), :]
    u_recv[h] = u_part[pl.ds(pl.multiple_of(h * chunk, chunk), chunk), :]
    each_line(lambda hq: remote(
        u_recv.at[hq], u_recv.at[hq], r_send.at[0], r_recv.at[hq], dev(h, p)).wait_recv())
    total = u_recv[0]
    for hs in range(1, line):
        total = total + u_recv[hs]

    own_diag.wait()
    u_out[u_at(h, p), :] = d_buf[...] + total

    def l_copy(hq):
        here = u_out.at[u_at(h, p)]
        return remote(here, here, l_send.at[hq], u_recv_sem.at[me], dev(hq, p))

    def u_copy(hs, k, q):
        here = u_out.at[u_at(hs, p)]
        return remote(here, here, u_send.at[hs, k], u_recv_sem.at[hs * group + p], dev(h, q))

    def n_copy(hs, k, q):
        here = u_out.at[u_at(hs, q)]
        return remote(here, here, n_send.at[hs, k], u_recv_sem.at[hs * group + q], dev(h, mate))

    def u_wait(hs, q):
        here = u_out.at[u_at(hs, q)]
        remote(here, here, l_send.at[0], u_recv_sem.at[hs * group + q], dev(h, p)).wait_recv()

    each_line(lambda hq: l_copy(hq).start())

    def spread(hs):
        each_chip(lambda k, q: u_copy(hs, k, q).start())
        n_copy(hs, 0, p).start()

    spread(h)

    def pass_on(hq):
        u_wait(hq, p)
        spread(hq)

    each_line(pass_on)

    each_plane(lambda k, q: remote(
        c_out.at[q], c_out.at[q], c_send.at[0], c_recv.at[q], dev(h, p)).wait_recv())
    for q in range(group):
        for s in range(per):
            x_buf[:, q * per + s, :] = c_out[q, :, s * sib_width:(s + 1) * sib_width]
    for b in range(rows // RB):
        panel_ref[b * RB:(b + 1) * RB] = -x_buf[b * RB:(b + 1) * RB] * mask_buf[b][None]

    def hand_over(hs):
        def one(k, q):
            u_wait(hs, q)
            n_copy(hs, k, q).start()
        each_chip(one)

    hand_over(h)
    each_line(hand_over)

    each_plane(lambda k, q: b_copy(k, q).wait_send())
    each_plane(lambda k, q: a_copy(k, q).wait_send())
    each_plane(lambda k, q: c_copy(k, q).wait_send())
    each_line(lambda hq: r_copy(hq).wait_send())
    each_line(lambda hq: l_copy(hq).wait_send())

    def drain(hs, carry):
        whole = b_buf.at[pl.ds(pl.multiple_of(hs * slab, slab), slab)]

        @pl.when((hs <= h) & (h + 1 < line))
        def _():
            remote(whole, whole, z_send.at[0, hs], b_recv.at[0], dev(h, p)).wait_send()

        @pl.when((hs >= h) & (h > 0))
        def _():
            remote(whole, whole, z_send.at[1, hs], b_recv.at[0], dev(h, p)).wait_send()

        n_copy(hs, 0, p).wait_send()
        each_chip(lambda k, q: u_copy(hs, k, q).wait_send())
        each_chip(lambda k, q: n_copy(hs, k, q).wait_send())
        u_wait(hs, mate)
        each_chip(lambda k, q: u_wait(hs, q + mate - p))
        return carry

    lax.fori_loop(0, line, drain, 0)


def leave(panel_in, update_in, panel_out, update_out, sem):
    first = pltpu.make_async_copy(update_in, update_out, sem.at[0])
    second = pltpu.make_async_copy(panel_in, panel_out, sem.at[1])
    first.start()
    second.start()
    first.wait()
    second.wait()


def per_device(row_devices, col_devices, ancestor, factor, diag_inv, structure):
    local_rows, count_sib, width = factor.shape
    lows = max(1, min(row_devices, count_sib // (2 * col_devices)))
    line, group = row_devices // lows, lows * col_devices
    per = count_sib // group
    chunk = per * width // line
    dma = pltpu.SemaphoreType.DMA
    vmem = pl.BlockSpec(memory_space=pltpu.VMEM)
    anywhere = pl.BlockSpec(memory_space=pl.ANY)
    f32 = jnp.float32
    panel, update = pl.pallas_call(
        functools.partial(kernel, line, group, lows, col_devices),
        out_shape=(
            pltpu.VMEM(factor.shape, f32),
            pltpu.VMEM((count_sib * width, width), f32),
        ),
        in_specs=[anywhere] * 4,
        out_specs=(vmem, vmem),
        scratch_shapes=[
            pltpu.VMEM(factor.shape, f32),
            pltpu.VMEM(structure.shape, structure.dtype),
            pltpu.VMEM((chunk, width), f32),
            pltpu.VMEM(factor.shape, f32),
            pltpu.VMEM((local_rows // RB, count_sib, width), f32),
            pltpu.VMEM((group, local_rows, per * width), f32),
            pltpu.VMEM((group, local_rows, per * width), f32),
            pltpu.VMEM((group,) + ancestor.shape, f32),
            pltpu.VMEM((line * group * local_rows, per * width), f32),
            pltpu.VMEM((group * local_rows, per * width), f32),
            pltpu.VMEM((per * width, width), f32),
            pltpu.VMEM((line, chunk, width), f32),
            dma((5,)), dma((group,)), dma((group,)), dma((group,)), dma((line * group,)),
            dma((2, line)), dma((group,)), dma((group,)), dma((line,)), dma((line,)),
            dma((line,)), dma((line, group // CORES)), dma((line, group // CORES)), dma((line * group,)),
        ],
        compiler_params=pltpu.CompilerParams(collective_id=0, has_side_effects=True),
    )(ancestor, factor, structure, diag_inv.reshape(count_sib * width, width))
    panel, update = pl.pallas_call(
        leave,
        out_shape=(
            jax.ShapeDtypeStruct(panel.shape, f32), jax.ShapeDtypeStruct(update.shape, f32),
        ),
        in_specs=[vmem] * 2,
        out_specs=(anywhere, anywhere),
        scratch_shapes=[dma((2,))],
    )(pltpu.with_memory_space_constraint(panel, pltpu.VMEM), pltpu.with_memory_space_constraint(update, pltpu.VMEM))
    return panel, update.reshape(count_sib, width, width)


def solution(mesh):
    placed = (P("row", "col"), P(("row", "col"), None, None), P(), P())
    return jax.shard_map(
        functools.partial(per_device, mesh.shape["row"], mesh.shape["col"]),
        mesh=mesh,
        in_specs=placed,
        out_specs=(P(("row", "col"), None, None), P()),
        check_vma=False,
    )
```
